128 devices in a mesh: dp: 8 (over z, core), label: 16 (over x, y).
Axes of the slice: x: 4, y: 4, z: 4, core: 2. Of those that a mesh axis runs over, the one named last changes fastest.
Arguments:
- features: bfloat16 [262144, 768], P(('dp', 'label')), may hold values from -6 to 6
- inst_ids: int32 [2048, 4], P(('dp', 'label')), may hold values from 0 to 15
- lab_ids: int32 [2048, 4], P(('dp', 'label')), may hold values from 0 to 15
- counts: int32 [2048], P(('dp', 'label')), may hold values from 0 to 4, as said below
- block_bits: int32 [2048, 4, 128, 128], P(('dp', 'label')), may hold values 0 or 1
- centroids: bfloat16 [2048, 768], P('label'), may hold values from -40 to 40
Outputs:
- label_embed: bfloat16 [32768, 768], P(('dp', 'label'))
- membership: bfloat16 [32768, 2048], P(('dp', 'label'))
- targets: bfloat16 [262144, 768], P(('dp', 'label'))
The draws below stay inside these ranges and needn't reach their ends.
Inputs may be any that keep to these rules, and one draw needn't show every extreme that they name: `lab_ids`: label block within the slot's label column. `counts`: in every draw one label column has all 4 slots used on every device.
All inputs are finite; a program needn't handle non-finite values. No bound on the sum of `block_bits` on one device may be relied on, other than what follows from the above.
Results may differ from the reference program's by a relative error of at most 0.008.
The reference program's roundings to bfloat16 on the way count: a program that leaves them out, or rounds other values in their place, can miss the bound.
Values may be sent and summed in bfloat16 or wider, within the bound.
No kernel may reach another device: no remote copies, remote signals or barrier semaphores. Data moves between devices by JAX's collectives and lax.ppermute only.
A program may use at most 128 MiB of HBM per device.

```python
import jax
import jax.numpy as jnp
from jax import lax

D = 768
NC = 2048
BLK = 128
CAP = 4
IB_DEV = 16
LB_DEV = 2
COLUMNS = 16
COL_BLOCKS = 16
SENDS = 2048
NI = 262144
LABELS = 32768
N_DP = 8
N_LABEL = 16


def draw_counts(key, part):
    drawn = jax.random.randint(key, (SENDS,), 0, CAP + 1)
    full_column = jax.random.randint(jax.random.fold_in(key, 7), (), 0, COLUMNS)
    column = jnp.arange(SENDS, dtype=jnp.int32) % COLUMNS
    return jnp.where(column == full_column, CAP, drawn).astype(jnp.int32)


def draw_centroids(key, part):
    normal = jnp.clip(jax.random.normal(key, (NC, D), jnp.float32), -5.0, 5.0)
    return (0.1 * normal).astype(jnp.bfloat16)


def set_ends(entries, rng, smallest, top_value):
    extent = entries.shape
    place = [jax.random.randint(jax.random.fold_in(rng, axis), (), 0, extent[axis]) for axis in range(len(extent))]
    entries = entries.at[tuple(place)].set(smallest)
    longest = extent.index(max(extent))
    place[longest] = (place[longest] + 1) % extent[longest]
    return entries.at[tuple(place)].set(top_value)


def block_scale(own_key, dims, pieces, least, high):
    gain = 1.0
    for position, shards_of in pieces:
        heights = jax.random.uniform(jax.random.fold_in(jax.random.fold_in(own_key, 6), position), (shards_of,), jnp.float32, least / len(pieces), high / len(pieces))
        gain = gain * jnp.repeat(jnp.exp(heights), dims[position] // shards_of).reshape((-1,) + (1,) * (len(dims) - 1 - position))
    return gain


def bell_draw(key, shape, scale, limit, cuts=(), kind=jnp.bfloat16):
    values = jax.random.normal(key, shape, jnp.float32) * scale
    if len(cuts) > 0:
        values = block_scale(key, shape, cuts, -0.22, 0.18) * values
    return jnp.clip(values, min=-limit, max=limit).astype(kind)


def setup_inputs(seed: int = 0) -> dict:
    streams_of = jax.random.split(jax.random.key(seed), 7)
    features = bell_draw(streams_of[0], (NI, D), 1.0, 6.0, ((0, 128),))
    inst_ids = set_ends(jax.random.randint(streams_of[1], (SENDS, CAP), 0, IB_DEV), jax.random.fold_in(streams_of[1], 1), 0, IB_DEV - 1).astype(jnp.int32)
    lab_ids = set_ends(jax.random.randint(streams_of[2], (SENDS, CAP), 0, COL_BLOCKS), jax.random.fold_in(streams_of[2], 1), 0, COL_BLOCKS - 1).astype(jnp.int32)
    counts = draw_counts(jax.random.fold_in(streams_of[6], 71), 0)
    block_bits = set_ends((jax.random.randint(streams_of[4], (SENDS, CAP, BLK, BLK), 0, 4) < 1).astype(jnp.int32), jax.random.fold_in(streams_of[4], 1), 0, 1)
    centroids = draw_centroids(jax.random.fold_in(streams_of[6], 71), 0)
    return dict(features=features, inst_ids=inst_ids, lab_ids=lab_ids, counts=counts, block_bits=block_bits, centroids=centroids)


epsilon = 1e-05

def global_blocks(lab_slots):
    column = jnp.arange(N_LABEL, dtype=jnp.int32)[:, None]
    return (lab_slots // LB_DEV * N_LABEL + column) * LB_DEV + lab_slots % LB_DEV

def reference(features, inst_ids, lab_ids, counts, block_bits, centroids):
    senders = N_DP * N_LABEL
    inst_blocks = features.reshape(senders, IB_DEV, BLK, D)
    inst_all = inst_ids.reshape(senders, N_LABEL, CAP)
    lab_all = lab_ids.reshape(senders, N_LABEL, CAP)
    count_all = counts.reshape(senders, N_LABEL)
    bits_all = block_bits.reshape(senders, N_LABEL, CAP, BLK, BLK)
    slot_index = jnp.arange(CAP, dtype=jnp.int32)

    def forward_step(totals, inputs):
        blocks, inst_slots, lab_slots, count_row, bits_row = inputs
        gathered = blocks[inst_slots]
        partials = jnp.einsum('ncab,ncad->ncbd', bits_row.astype(jnp.float32), gathered.astype(jnp.float32))
        partials = lax.optimization_barrier(partials.astype(jnp.bfloat16)).astype(jnp.float32)
        filled = slot_index[None, :] < count_row[:, None]
        partials = jnp.where(filled[:, :, None, None], partials, jnp.zeros_like(partials))
        targets_idx = global_blocks(lab_slots).reshape(-1)
        totals = totals.at[targets_idx].add(partials.reshape(-1, BLK, D))
        return (totals, None)
    start = jnp.zeros((senders * LB_DEV, BLK, D), jnp.float32)
    totals, unused = lax.scan(forward_step, start, (inst_blocks, inst_all, lab_all, count_all, bits_all))
    aggregate = totals.reshape(LABELS, D)
    embed32 = aggregate * lax.rsqrt(lax.optimization_barrier(jnp.mean(aggregate * aggregate, axis=1, keepdims=True)) + epsilon)
    label_embed = embed32.astype(jnp.bfloat16)
    scores = jnp.dot(label_embed, centroids.T, preferred_element_type=jnp.float32)
    row_peak = lax.optimization_barrier(jnp.max(scores, axis=1, keepdims=True))
    lifted = jnp.exp(scores - row_peak)
    membership = (lifted / lax.optimization_barrier(jnp.sum(lifted, axis=1, keepdims=True))).astype(jnp.bfloat16)
    mixed = jnp.dot(membership, centroids, preferred_element_type=jnp.float32).astype(jnp.bfloat16)
    mixed_blocks = mixed.reshape(senders * LB_DEV, BLK, D)

    def reverse_step(inputs):
        inst_slots, lab_slots, count_row, bits_row = inputs
        picked = mixed_blocks[global_blocks(lab_slots)]
        filled = slot_index[None, :] < count_row[:, None]
        picked = jnp.where(filled[:, :, None, None], picked.astype(jnp.float32), jnp.zeros(picked.shape, jnp.float32))
        contrib = jnp.einsum('ncab,ncbd->ncad', bits_row.astype(jnp.float32), picked)
        raw = jnp.zeros((IB_DEV, BLK, D), jnp.float32)
        return raw.at[inst_slots.reshape(-1)].add(contrib.reshape(-1, BLK, D))
    raw_targets = lax.map(reverse_step, (inst_all, lab_all, count_all, bits_all)).reshape(NI, D)
    targets = raw_targets * lax.rsqrt(lax.optimization_barrier(jnp.mean(raw_targets * raw_targets, axis=1, keepdims=True)) + epsilon)
    return (label_embed, membership, targets.astype(jnp.bfloat16))
```

```python
import functools

import jax
import jax.numpy as jnp
from jax import lax
from jax.experimental import pallas as pl
from jax.experimental.pallas import tpu as pltpu
from jax.sharding import PartitionSpec as P

LB_DEV = 2
EPSILON = 1e-05
CHUNKS = 1


def partial_kernel(cap, inst_ref, count_ref, bits_ref, feat_ref, out_ref):
    column = pl.program_id(0)
    block = bits_ref.shape[-1]
    for k in range(cap):

        @pl.when(k < count_ref[column])
        def _():
            incidence = bits_ref[0, k].astype(jnp.float32).astype(jnp.bfloat16)
            rows = feat_ref[inst_ref[column * cap + k]]
            part = lax.dot_general(
                incidence, rows, (((0,), (0,)), ((), ())), preferred_element_type=jnp.float32
            )
            out_ref[0, k * block : (k + 1) * block] = part.astype(jnp.bfloat16)


def partial_blocks(inst_flat, counts, block_bits, inst_blocks, chunk, width):
    columns, cap, block, _ = block_bits.shape
    n_inst = inst_blocks.shape[0]
    return pl.pallas_call(
        functools.partial(partial_kernel, cap),
        out_shape=jax.ShapeDtypeStruct((columns, cap * block, width), jnp.bfloat16),
        grid_spec=pltpu.PrefetchScalarGridSpec(
            num_scalar_prefetch=2,
            grid=(columns,),
            in_specs=[
                pl.BlockSpec((1, cap, block, block), lambda c, i, n: (c, 0, 0, 0)),
                pl.BlockSpec((n_inst, block, width), lambda c, i, n: (0, 0, chunk)),
            ],
            out_specs=pl.BlockSpec((1, cap * block, width), lambda c, i, n: (c, 0, 0)),
        ),
        name="partial_blocks",
    )(inst_flat, counts, block_bits, inst_blocks)


def sum_kernel(cap, ids_ref, arrived_ref, out_ref):
    sender = pl.program_id(0)
    block = out_ref.shape[1]

    @pl.when(sender == 0)
    def _():
        out_ref[...] = jnp.zeros_like(out_ref)

    for k in range(cap):
        target = ids_ref[sender * cap + k]

        @pl.when(target >= 0)
        def _():
            out_ref[target] += arrived_ref[0, k * block : (k + 1) * block].astype(jnp.float32)


def sum_blocks(flat_ids, arrived, col_blocks, block):
    senders, rows, width = arrived.shape
    cap = rows // block
    return pl.pallas_call(
        functools.partial(sum_kernel, cap),
        out_shape=jax.ShapeDtypeStruct((col_blocks, block, width), jnp.float32),
        grid_spec=pltpu.PrefetchScalarGridSpec(
            num_scalar_prefetch=1,
            grid=(senders,),
            in_specs=[pl.BlockSpec((1, rows, width), lambda e, ids: (e, 0, 0))],
            out_specs=pl.BlockSpec((col_blocks, block, width), lambda e, ids: (0, 0, 0)),
        ),
        name="sum_blocks",
    )(flat_ids, arrived)


def label_kernel(pieces, *refs):
    sum_refs, (cent_ref, embed_ref, member_ref, mixed_ref) = refs[:pieces], refs[pieces:]
    sums = [ref[...] for ref in sum_refs]
    sums = sums[0] if pieces == 1 else jnp.concatenate(sums, axis=1)
    embed = (sums * lax.rsqrt(jnp.mean(sums * sums, axis=1, keepdims=True) + EPSILON)).astype(jnp.bfloat16)
    embed_ref[...] = embed
    scores = lax.dot_general(embed, cent_ref[...], (((1,), (1,)), ((), ())), preferred_element_type=jnp.float32)
    lifted = jnp.exp(scores - jnp.max(scores, axis=1, keepdims=True))
    member = (lifted / jnp.sum(lifted, axis=1, keepdims=True)).astype(jnp.bfloat16)
    member_ref[...] = member
    mixed_ref[...] = jnp.dot(member, cent_ref[...], preferred_element_type=jnp.float32).astype(jnp.bfloat16)


def label_side(sums, centroids):
    rows = sums[0].shape[0]
    clusters, feat = centroids.shape
    tile = 128
    by_row = lambda i: (i, 0)
    return pl.pallas_call(
        functools.partial(label_kernel, len(sums)),
        out_shape=(
            jax.ShapeDtypeStruct((rows, feat), jnp.bfloat16),
            jax.ShapeDtypeStruct((rows, clusters), jnp.bfloat16),
            jax.ShapeDtypeStruct((rows, feat), jnp.bfloat16),
        ),
        grid=(rows // tile,),
        in_specs=[pl.BlockSpec((tile, s.shape[1]), by_row) for s in sums]
        + [pl.BlockSpec((clusters, feat), lambda i: (0, 0))],
        out_specs=(
            pl.BlockSpec((tile, feat), by_row),
            pl.BlockSpec((tile, clusters), by_row),
            pl.BlockSpec((tile, feat), by_row),
        ),
        name="label_side",
    )(*sums, centroids)


def target_kernel(cap, inst_ref, lab_ref, count_ref, bits_ref, *refs):
    mixed_refs, (out_ref, total) = refs[:cap], refs[cap:]
    column = pl.program_id(0)

    @pl.when(column == 0)
    def _():
        total[...] = jnp.zeros_like(total)

    for k in range(cap):

        @pl.when(k < count_ref[column])
        def _():
            incidence = bits_ref[0, k].astype(jnp.float32).astype(jnp.bfloat16)
            part = jnp.dot(incidence, mixed_refs[k][0], preferred_element_type=jnp.float32)
            total[inst_ref[column * cap + k]] += part

    @pl.when(column == pl.num_programs(0) - 1)
    def _():
        for g in range(total.shape[0]):
            raw = total[g]
            scale = lax.rsqrt(jnp.mean(raw * raw, axis=1, keepdims=True) + EPSILON)
            out_ref[g] = (raw * scale).astype(jnp.bfloat16)


def target_blocks(inst_flat, lab_flat, counts, block_bits, mixed_blocks, n_inst):
    columns, cap, block, _ = block_bits.shape
    feat = mixed_blocks.shape[-1]
    picked = [
        pl.BlockSpec((1, block, feat), lambda c, i, h, n, k=k: (h[c * cap + k], 0, 0)) for k in range(cap)
    ]
    return pl.pallas_call(
        functools.partial(target_kernel, cap),
        out_shape=jax.ShapeDtypeStruct((n_inst, block, feat), jnp.bfloat16),
        grid_spec=pltpu.PrefetchScalarGridSpec(
            num_scalar_prefetch=3,
            grid=(columns,),
            in_specs=[pl.BlockSpec((1, cap, block, block), lambda c, i, h, n: (c, 0, 0, 0))] + picked,
            out_specs=pl.BlockSpec((n_inst, block, feat), lambda c, i, h, n: (0, 0, 0)),
            scratch_shapes=[pltpu.VMEM((n_inst, block, feat), jnp.float32)],
        ),
        name="target_blocks",
    )(inst_flat, lab_flat, counts, block_bits, *([mixed_blocks] * cap))


def body(features, inst_ids, lab_ids, counts, block_bits, centroids):
    columns, cap = inst_ids.shape
    block = block_bits.shape[-1]
    feat = features.shape[1]
    inst_blocks = features.reshape(-1, block, feat)
    inst_flat = inst_ids.reshape(-1)
    filled = jnp.arange(cap)[None, :] < counts[:, None]
    tagged_ids = jnp.where(filled, lab_ids, -1)
    all_ids = lax.all_gather(tagged_ids, "label", axis=0, tiled=False)
    all_rows = lax.all_gather(centroids, "label", axis=0, tiled=True)
    arrived_ids = lax.dynamic_index_in_dim(all_ids, lax.axis_index("label"), axis=1, keepdims=False)
    flat_ids = arrived_ids.reshape(-1)
    col_blocks = lax.axis_size("dp") * LB_DEV

    width = feat // CHUNKS
    sums = []
    for chunk in range(CHUNKS):
        partials = partial_blocks(inst_flat, counts, block_bits, inst_blocks, chunk, width)
        arrived = lax.all_to_all(partials, "label", split_axis=0, concat_axis=0, tiled=True)
        column_sums = sum_blocks(flat_ids, arrived, col_blocks, block)
        sums.append(
            lax.psum_scatter(
                column_sums.reshape(col_blocks * block, width), "dp", scatter_dimension=0, tiled=True
            )
        )
    label_embed, membership, mixed = label_side(sums, all_rows)
    mixed_all = lax.all_gather(mixed, ("dp", "label"), axis=0, tiled=True)
    column = jnp.arange(columns, dtype=jnp.int32)[:, None]
    global_ids = (lab_ids // LB_DEV * columns + column) * LB_DEV + lab_ids % LB_DEV
    targets = target_blocks(
        inst_flat, global_ids.reshape(-1), counts, block_bits, mixed_all.reshape(-1, block, feat), inst_blocks.shape[0]
    )
    return (label_embed, membership, targets.reshape(features.shape))


def solution(mesh):
    in_specs = (
        P(("dp", "label"), None),
        P(("dp", "label"), None),
        P(("dp", "label"), None),
        P(("dp", "label")),
        P(("dp", "label"), None, None, None),
        P("label", None),
    )
    out_specs = (P(("dp", "label"), None), P(("dp", "label"), None), P(("dp", "label"), None))
    return jax.shard_map(body, mesh=mesh, in_specs=in_specs, out_specs=out_specs, check_vma=False)
```

```python
import functools

import jax
import jax.numpy as jnp
from jax import lax
from jax.experimental import pallas as pl
from jax.experimental.pallas import tpu as pltpu
from jax.sharding import PartitionSpec as P


LB_DEV = 2
EPSILON = 1e-05
SUM_STEPS = 2
LABEL_TILE = 256
TARGET_GROUP = 8
SIDE = 4
SPLITS = ((256, 0), (128, 4))


MAKE = (
    (0, ((0, 1),)),
    (0, ((1, 1),)),
    (0, ((0, 3), (0, 2))),
    (0, ((1, 3), (1, 2))),
    (1, ((0, 1), (0, 3), (0, 2))),
    (1, ((1, 1), (1, 3), (1, 2))),
    (0, ((0, 0), (1, 0))),
    (1, ((0, 0), (1, 0))),
)


def mod4(value):
    return jnp.bitwise_and(value, SIDE - 1)


def shift_first(array, step):
    pairs = [(a * SIDE + b, (a + step) % SIDE * SIDE + b) for a in range(SIDE) for b in range(SIDE)]
    return lax.ppermute(array, "label", pairs)


def shift_second(array, step):
    pairs = [(a * SIDE + b, a * SIDE + (b + step) % SIDE) for a in range(SIDE) for b in range(SIDE)]
    return lax.ppermute(array, "label", pairs)


def shift_plane(array, step):
    pairs = [(a * 2 + b, (a + step) % SIDE * 2 + b) for a in range(SIDE) for b in range(2)]
    return lax.ppermute(array, "dp", pairs)


def swap_core(array):
    return lax.ppermute(array, "dp", [(a * 2 + b, a * 2 + 1 - b) for a in range(SIDE) for b in range(2)])


def partial_kernel(cap, groups, axes, pos_ref, inst_ref, *refs):
    bits_refs, refs = refs[: len(groups)], refs[len(groups) :]
    feat_refs, out_refs = dict(zip(axes, refs)), refs[len(axes) :]
    for (first_axis, outer), bits_ref, out_ref in zip(groups, bits_refs, out_refs):
        fixed = mod4(pos_ref[first_axis] + outer)
        for inner in range(SIDE):
            other = mod4(pos_ref[1 - first_axis] + inner)
            column = fixed * SIDE + other if first_axis == 0 else other * SIDE + fixed
            for k in range(cap):
                incidence = bits_ref[0, other, k] if first_axis == 0 else bits_ref[other, 0, k]
                part = lax.dot_general(
                    incidence.astype(jnp.float32).astype(jnp.bfloat16),
                    feat_refs[first_axis][inst_ref[column * cap + k]],
                    (((0,), (0,)), ((), ())),
                    preferred_element_type=jnp.float32,
                )
                out_ref[inner, k] = part.astype(jnp.bfloat16)


def partial_blocks(pos, inst_flat, block_bits, inst_blocks, groups, part):
    _, cap, block, _ = block_bits.shape
    n_inst = inst_blocks.shape[0]
    width, start = SPLITS[part]
    grid_bits = block_bits.reshape(SIDE, SIDE, cap, block, block)
    axes = tuple(sorted({first_axis for first_axis, _ in groups}))
    bits_specs = []
    for first_axis, outer in groups:
        if first_axis == 0:
            shape, index = (1, SIDE), lambda g, p, i, outer=outer: (mod4(p[0] + outer), 0, 0, 0, 0)
        else:
            shape, index = (SIDE, 1), lambda g, p, i, outer=outer: (0, mod4(p[1] + outer), 0, 0, 0)
        bits_specs.append(pl.BlockSpec(shape + (cap, block, block), index))
    feat_specs = [
        pl.BlockSpec((n_inst, block, width), lambda g, p, i, at=start + axis: (0, 0, at)) for axis in axes
    ]
    out = jax.ShapeDtypeStruct((SIDE, cap, block, width), jnp.bfloat16)
    return pl.pallas_call(
        functools.partial(partial_kernel, cap, groups, axes),
        out_shape=(out,) * len(groups),
        grid_spec=pltpu.PrefetchScalarGridSpec(
            num_scalar_prefetch=2,
            grid=(1,),
            in_specs=bits_specs + feat_specs,
            out_specs=(pl.BlockSpec(out.shape, lambda g, p, i: (0, 0, 0, 0)),) * len(groups),
        ),
        cost_estimate=pl.CostEstimate(
            flops=2 * len(groups) * SIDE * cap * block * block * width,
            bytes_accessed=len(groups) * (4 << 20),
            transcendentals=0,
        ),
        name="partial_blocks",
    )(pos, inst_flat, *([grid_bits] * len(groups)), *([inst_blocks] * len(axes)))


def pack_kernel(*refs):
    ins, outs = refs[:SIDE], refs[SIDE:]
    for outer, out_ref in enumerate(outs, start=1):
        for step, ref in enumerate(ins):
            out_ref[step] = ref[outer]


def pack_groups(received):
    shape = received[0].shape
    whole = pl.BlockSpec(shape, lambda i: (0, 0, 0, 0))
    return pl.pallas_call(
        pack_kernel,
        out_shape=(jax.ShapeDtypeStruct(shape, received[0].dtype),) * (SIDE - 1),
        grid=(1,),
        in_specs=[whole] * len(received),
        out_specs=(whole,) * (SIDE - 1),
        cost_estimate=pl.CostEstimate(flops=0, bytes_accessed=8 << 20, transcendentals=0),
        name="pack_groups",
    )(*received)


def sum_kernel(cap, width, pos_ref, ids_ref, *refs):
    arrived, (keep_ref, send_ref, total) = refs[: 4 * SIDE - 2], refs[4 * SIDE - 2 :]
    half = keep_ref.shape[0]
    per_step = SIDE // SUM_STEPS
    at = pl.program_id(0) * per_step

    @pl.when(at == 0)
    def _():
        total[...] = jnp.zeros_like(total)

    def add(first_axis, outer, inner, ref, row_at):
        step = (inner, outer) if first_axis == 0 else (outer, inner)
        sender = step[0] * SIDE + step[1]
        for k in range(cap):
            target = ids_ref[sender * cap + k]

            @pl.when(target >= 0)
            def _():
                away = jnp.bitwise_xor(jnp.bitwise_and(target >> 1, 1), pos_ref[3])
                row = away * half + mod4((target >> 2) - pos_ref[2]) * LB_DEV + jnp.bitwise_and(target, 1)
                columns = pl.ds(first_axis * width, width)
                total[row, :, columns] += ref[row_at, k].astype(jnp.float32)

    for first_axis in range(2):
        refs_here = arrived[first_axis * (2 * SIDE - 1) : (first_axis + 1) * (2 * SIDE - 1)]
        for step in range(SIDE):

            @pl.when(at == step // per_step * per_step)
            def _():
                add(first_axis, 0, step, refs_here[step], 0)

        for outer in range(1, SIDE):
            for step in range(per_step):
                add(first_axis, outer, at + step, refs_here[SIDE - 1 + outer], step)

    @pl.when(at == SIDE - per_step)
    def _():
        keep_ref[...] = total[:half]
        send_ref[...] = total[half:]


def sum_blocks(pos, flat_ids, arrived, col_blocks):
    _, cap, block, width = arrived[0].shape
    half = jax.ShapeDtypeStruct((col_blocks // 2, block, 2 * width), jnp.float32)
    whole = pl.BlockSpec(half.shape, lambda j, p, i: (0, 0, 0))
    own = pl.BlockSpec((1, cap, block, width), lambda j, p, i: (0, 0, 0, 0))
    far = pl.BlockSpec((SIDE // SUM_STEPS, cap, block, width), lambda j, p, i: (j, 0, 0, 0))
    return pl.pallas_call(
        functools.partial(sum_kernel, cap, width),
        out_shape=(half, half),
        grid_spec=pltpu.PrefetchScalarGridSpec(
            num_scalar_prefetch=2,
            grid=(SUM_STEPS,),
            in_specs=([own] * SIDE + [far] * (SIDE - 1)) * 2,
            out_specs=(whole, whole),
            scratch_shapes=[pltpu.VMEM((col_blocks, block, 2 * width), jnp.float32)],
        ),
        cost_estimate=pl.CostEstimate(
            flops=SIDE * SIDE * cap * block * 2 * width, bytes_accessed=12 << 20, transcendentals=0
        ),
        name="sum_blocks",
    )(pos, flat_ids, *arrived)


def label_kernel(*refs):
    sum_refs, (cent_ref, embed_ref, member_ref, mixed_ref) = refs[:-4], refs[-4:]
    sums = []
    for at in range(0, len(sum_refs), SIDE):
        sums.append(sum_refs[at][...] + sum_refs[at + 1][...] + sum_refs[at + 2][...] + sum_refs[at + 3][...])
    sums = jnp.concatenate(sums, axis=1)
    embed = (sums * lax.rsqrt(jnp.mean(sums * sums, axis=1, keepdims=True) + EPSILON)).astype(jnp.bfloat16)
    embed_ref[...] = embed
    scores = lax.dot_general(embed, cent_ref[...], (((1,), (1,)), ((), ())), preferred_element_type=jnp.float32)
    lifted = jnp.exp(scores - jnp.max(scores, axis=1, keepdims=True))
    member = (lifted / jnp.sum(lifted, axis=1, keepdims=True)).astype(jnp.bfloat16)
    member_ref[...] = member
    mixed_ref[...] = jnp.dot(member, cent_ref[...], preferred_element_type=jnp.float32).astype(jnp.bfloat16)


def label_side(sums, centroids):
    rows = sums[0].shape[0]
    clusters, feat = centroids.shape
    tile = LABEL_TILE
    by_row = lambda i: (i, 0)
    return pl.pallas_call(
        label_kernel,
        out_shape=(
            jax.ShapeDtypeStruct((rows, feat), jnp.bfloat16),
            jax.ShapeDtypeStruct((rows, clusters), jnp.bfloat16),
            jax.ShapeDtypeStruct((rows, feat), jnp.bfloat16),
        ),
        grid=(rows // tile,),
        in_specs=[pl.BlockSpec((tile, s.shape[1]), by_row) for s in sums]
        + [pl.BlockSpec((clusters, feat), lambda i: (0, 0))],
        out_specs=(
            pl.BlockSpec((tile, feat), by_row),
            pl.BlockSpec((tile, clusters), by_row),
            pl.BlockSpec((tile, feat), by_row),
        ),
        name="label_side",
    )(*sums, centroids)


def target_kernel(group, count_ref, slot_ref, inst_ref, lab_ref, *refs):
    bits_refs, mixed_refs, (out_ref, total) = refs[:group], refs[group : 2 * group], refs[2 * group :]
    at = pl.program_id(0) * group

    @pl.when(at == 0)
    def _():
        total[...] = jnp.zeros_like(total)

    @pl.when(at < count_ref[0])
    def _():
        for k in range(group):
            used = (at + k < count_ref[0]).astype(jnp.int32)
            incidence = (bits_refs[k][0] * used).astype(jnp.float32).astype(jnp.bfloat16)
            part = jnp.dot(incidence, mixed_refs[k][0], preferred_element_type=jnp.float32)
            total[inst_ref[at + k]] += part

    @pl.when(at + group == group * pl.num_programs(0))
    def _():
        for g in range(total.shape[0]):
            raw = total[g]
            scale = lax.rsqrt(jnp.mean(raw * raw, axis=1, keepdims=True) + EPSILON)
            out_ref[g] = (raw * scale).astype(jnp.bfloat16)


def target_blocks(slots, insts, labs, n_used, block_bits, mixed_blocks, n_inst):
    n_slots, block, _ = block_bits.shape
    feat = mixed_blocks.shape[-1]
    group = TARGET_GROUP

    def pick(table, k):
        def index(g, n, *tables):
            return (tables[table][jnp.minimum(g, (jnp.maximum(n[0], 1) - 1) // group) * group + k], 0, 0)

        return index

    return pl.pallas_call(
        functools.partial(target_kernel, group),
        out_shape=jax.ShapeDtypeStruct((n_inst, block, feat), jnp.bfloat16),
        grid_spec=pltpu.PrefetchScalarGridSpec(
            num_scalar_prefetch=4,
            grid=(n_slots // group,),
            in_specs=[pl.BlockSpec((1, block, block), pick(0, k)) for k in range(group)]
            + [pl.BlockSpec((1, block, feat), pick(2, k)) for k in range(group)],
            out_specs=pl.BlockSpec((n_inst, block, feat), lambda g, *tables: (0, 0, 0)),
            scratch_shapes=[pltpu.VMEM((n_inst, block, feat), jnp.float32)],
        ),
        name="target_blocks",
    )(n_used, slots, insts, labs, *([block_bits] * group), *([mixed_blocks] * group))


def body(features, inst_ids, lab_ids, counts, block_bits, centroids):
    columns, cap = inst_ids.shape
    block = block_bits.shape[-1]
    feat = features.shape[1]
    planes = lax.axis_size("dp")
    inst_blocks = features.reshape(-1, block, feat)
    inst_flat = inst_ids.reshape(-1)
    d = lax.axis_index("dp")
    e = lax.axis_index("label")
    pos = jnp.stack([e // SIDE, e % SIDE, d // 2, d % 2]).astype(jnp.int32)

    filled = jnp.arange(cap)[None, :] < counts[:, None]
    tagged_ids = jnp.where(filled, lab_ids, -1).reshape(SIDE, SIDE, cap)
    tagged_ids = jnp.roll(tagged_ids, (-(e // SIDE), -(e % SIDE)), (0, 1))
    near = [shift_first(tagged_ids[step], step) if step else tagged_ids[0] for step in range(SIDE)]
    near = jnp.stack(near, axis=1)
    near = [shift_second(near[step], step) if step else near[0] for step in range(SIDE)]
    flat_ids = jnp.stack(near, axis=1).reshape(-1)

    share = centroids.shape[0] // planes
    own_rows = lax.dynamic_slice_in_dim(centroids, d * share, share, 0)
    all_rows = lax.all_gather(own_rows, ("label", "dp"), axis=0, tiled=True)

    shifts = (shift_first, shift_second)
    sums = []
    stage = {}
    for part, groups in MAKE:
        made = partial_blocks(pos, inst_flat, block_bits, inst_blocks, groups, part)
        for (first_axis, outer), blocks in zip(groups, made):
            stage[part, first_axis, outer] = shifts[first_axis](blocks, outer) if outer else blocks
    for part in range(len(SPLITS)):
        arrived = []
        for first_axis in range(2):
            received = [stage[part, first_axis, step] for step in range(SIDE)]
            arrived += received
            packed = pack_groups(received)
            for outer, group in enumerate(packed, start=1):
                arrived.append(shifts[1 - first_axis](group, outer))
        keep, send = sum_blocks(pos, flat_ids, arrived, planes * LB_DEV)
        other = swap_core(send)
        for step in range(SIDE):
            rows = slice(step * LB_DEV, (step + 1) * LB_DEV)
            piece = (keep[rows] + other[rows]).reshape(LB_DEV * block, -1)
            sums.append(shift_plane(piece, step) if step else piece)
    label_embed, membership, mixed = label_side(sums, all_rows)
    mixed_all = lax.all_gather(mixed, ("dp", "label"), axis=0, tiled=True)

    column = jnp.arange(columns, dtype=jnp.int32)[:, None]
    global_ids = ((lab_ids // LB_DEV * columns + column) * LB_DEV + lab_ids % LB_DEV).reshape(-1)
    used = filled.reshape(-1)
    place = jnp.where(used, jnp.cumsum(used) - 1, used.size)
    slots = jnp.arange(used.size, dtype=jnp.int32)
    chosen = (place[None, :] == slots[:, None]).astype(jnp.int32)
    tables = [jnp.sum(chosen * table[None, :], axis=1) for table in (slots, inst_flat, global_ids)]
    n_used = jnp.sum(used, dtype=jnp.int32).reshape(1)
    targets = target_blocks(
        *tables, n_used, block_bits.reshape(-1, block, block), mixed_all.reshape(-1, block, feat), inst_blocks.shape[0]
    )
    return (label_embed, membership, targets.reshape(features.shape))


def solution(mesh):
    in_specs = (
        P(("dp", "label"), None),
        P(("dp", "label"), None),
        P(("dp", "label"), None),
        P(("dp", "label")),
        P(("dp", "label"), None, None, None),
        P("label", None),
    )
    out_specs = (P(("dp", "label"), None), P(("dp", "label"), None), P(("dp", "label"), None))
    return jax.shard_map(body, mesh=mesh, in_specs=in_specs, out_specs=out_specs, check_vma=False)
```

```python
import functools

import jax
import jax.numpy as jnp
from jax import lax
from jax.experimental import pallas as pl
from jax.experimental.pallas import tpu as pltpu
from jax.sharding import PartitionSpec as P


LB_DEV = 2
EPSILON = 1e-05
SUM_STEPS = 2
LABEL_TILE = 256
TARGET_GROUP = 8
SIDE = 4
SPLITS = ((256, 0), (128, 4))


MAKE = (
    (0, ((0, 2),)),
    (0, ((1, 2),)),
    (0, ((0, 1), (0, 3))),
    (0, ((1, 1), (1, 3))),
    (1, ((0, 2), (0, 1), (0, 3))),
    (1, ((1, 2), (1, 1), (1, 3))),
    (0, ((0, 0), (1, 0))),
    (1, ((0, 0), (1, 0))),
)


def mod4(value):
    return jnp.bitwise_and(value, SIDE - 1)


def shift_first(array, step):
    pairs = [(a * SIDE + b, (a + step) % SIDE * SIDE + b) for a in range(SIDE) for b in range(SIDE)]
    return lax.ppermute(array, "label", pairs)


def shift_second(array, step):
    pairs = [(a * SIDE + b, a * SIDE + (b + step) % SIDE) for a in range(SIDE) for b in range(SIDE)]
    return lax.ppermute(array, "label", pairs)


def shift_plane(array, step):
    pairs = [(a * 2 + b, (a + step) % SIDE * 2 + b) for a in range(SIDE) for b in range(2)]
    return lax.ppermute(array, "dp", pairs)


def swap_core(array):
    return lax.ppermute(array, "dp", [(a * 2 + b, a * 2 + 1 - b) for a in range(SIDE) for b in range(2)])


def partial_kernel(cap, groups, axes, pos_ref, inst_ref, *refs):
    bits_refs, refs = refs[: len(groups)], refs[len(groups) :]
    feat_refs, out_refs = dict(zip(axes, refs)), refs[len(axes) :]
    for (first_axis, outer), bits_ref, out_ref in zip(groups, bits_refs, out_refs):
        fixed = mod4(pos_ref[first_axis] + outer)
        for inner in range(SIDE):
            other = mod4(pos_ref[1 - first_axis] + inner)
            column = fixed * SIDE + other if first_axis == 0 else other * SIDE + fixed
            for k in range(cap):
                incidence = bits_ref[0, other, k] if first_axis == 0 else bits_ref[other, 0, k]
                part = lax.dot_general(
                    incidence.astype(jnp.float32).astype(jnp.bfloat16),
                    feat_refs[first_axis][inst_ref[column * cap + k]],
                    (((0,), (0,)), ((), ())),
                    preferred_element_type=jnp.float32,
                )
                out_ref[inner, k] = part.astype(jnp.bfloat16)


def partial_blocks(pos, inst_flat, block_bits, inst_blocks, groups, part):
    _, cap, block, _ = block_bits.shape
    n_inst = inst_blocks.shape[0]
    width, start = SPLITS[part]
    grid_bits = block_bits.reshape(SIDE, SIDE, cap, block, block)
    axes = tuple(sorted({first_axis for first_axis, _ in groups}))
    bits_specs = []
    for first_axis, outer in groups:
        if first_axis == 0:
            shape, index = (1, SIDE), lambda g, p, i, outer=outer: (mod4(p[0] + outer), 0, 0, 0, 0)
        else:
            shape, index = (SIDE, 1), lambda g, p, i, outer=outer: (0, mod4(p[1] + outer), 0, 0, 0)
        bits_specs.append(pl.BlockSpec(shape + (cap, block, block), index))
    feat_specs = [
        pl.BlockSpec((n_inst, block, width), lambda g, p, i, at=start + axis: (0, 0, at)) for axis in axes
    ]
    out = jax.ShapeDtypeStruct((SIDE, cap, block, width), jnp.bfloat16)
    return pl.pallas_call(
        functools.partial(partial_kernel, cap, groups, axes),
        out_shape=(out,) * len(groups),
        grid_spec=pltpu.PrefetchScalarGridSpec(
            num_scalar_prefetch=2,
            grid=(1,),
            in_specs=bits_specs + feat_specs,
            out_specs=(pl.BlockSpec(out.shape, lambda g, p, i: (0, 0, 0, 0)),) * len(groups),
        ),
        cost_estimate=pl.CostEstimate(
            flops=2 * len(groups) * SIDE * cap * block * block * width,
            bytes_accessed=len(groups) * (4 << 20),
            transcendentals=0,
        ),
        name="partial_blocks",
    )(pos, inst_flat, *([grid_bits] * len(groups)), *([inst_blocks] * len(axes)))


def pack_kernel(*refs):
    ins, outs = refs[:SIDE], refs[SIDE:]
    for outer, out_ref in enumerate(outs, start=1):
        for step, ref in enumerate(ins):
            out_ref[step] = ref[outer]


def pack_groups(received):
    shape = received[0].shape
    whole = pl.BlockSpec(shape, lambda i: (0, 0, 0, 0))
    return pl.pallas_call(
        pack_kernel,
        out_shape=(jax.ShapeDtypeStruct(shape, received[0].dtype),) * (SIDE - 1),
        grid=(1,),
        in_specs=[whole] * len(received),
        out_specs=(whole,) * (SIDE - 1),
        cost_estimate=pl.CostEstimate(flops=0, bytes_accessed=8 << 20, transcendentals=0),
        name="pack_groups",
    )(*received)


def sum_kernel(cap, width, pos_ref, ids_ref, *refs):
    arrived, (keep_ref, send_ref, total) = refs[: 4 * SIDE - 2], refs[4 * SIDE - 2 :]
    half = keep_ref.shape[0]
    per_step = SIDE // SUM_STEPS
    at = pl.program_id(0) * per_step

    @pl.when(at == 0)
    def _():
        total[...] = jnp.zeros_like(total)

    def add(first_axis, outer, inner, ref, row_at):
        step = (inner, outer) if first_axis == 0 else (outer, inner)
        sender = step[0] * SIDE + step[1]
        for k in range(cap):
            target = ids_ref[sender * cap + k]
            away = jnp.bitwise_xor(jnp.bitwise_and(target >> 1, 1), pos_ref[3])
            row = away * half + mod4((target >> 2) - pos_ref[2]) * LB_DEV + jnp.bitwise_and(target, 1)
            row = jnp.where(target >= 0, row, 2 * half)
            columns = pl.ds(first_axis * width, width)
            total[row, :, columns] += ref[row_at, k].astype(jnp.float32)

    for first_axis in range(2):
        refs_here = arrived[first_axis * (2 * SIDE - 1) : (first_axis + 1) * (2 * SIDE - 1)]
        for step in range(SIDE):

            @pl.when(at == step // per_step * per_step)
            def _():
                add(first_axis, 0, step, refs_here[step], 0)

        for outer in range(1, SIDE):
            for step in range(per_step):
                add(first_axis, outer, at + step, refs_here[SIDE - 1 + outer], step)

    @pl.when(at == SIDE - per_step)
    def _():
        keep_ref[...] = total[:half]
        send_ref[...] = total[half : 2 * half]


def sum_blocks(pos, flat_ids, arrived, col_blocks):
    _, cap, block, width = arrived[0].shape
    half = jax.ShapeDtypeStruct((col_blocks // 2, block, 2 * width), jnp.float32)
    whole = pl.BlockSpec(half.shape, lambda j, p, i: (0, 0, 0))
    own = pl.BlockSpec((1, cap, block, width), lambda j, p, i: (0, 0, 0, 0))
    far = pl.BlockSpec((SIDE // SUM_STEPS, cap, block, width), lambda j, p, i: (j, 0, 0, 0))
    return pl.pallas_call(
        functools.partial(sum_kernel, cap, width),
        out_shape=(half, half),
        grid_spec=pltpu.PrefetchScalarGridSpec(
            num_scalar_prefetch=2,
            grid=(SUM_STEPS,),
            in_specs=([own] * SIDE + [far] * (SIDE - 1)) * 2,
            out_specs=(whole, whole),
            scratch_shapes=[pltpu.VMEM((col_blocks + 1, block, 2 * width), jnp.float32)],
        ),
        cost_estimate=pl.CostEstimate(
            flops=SIDE * SIDE * cap * block * 2 * width, bytes_accessed=12 << 20, transcendentals=0
        ),
        name="sum_blocks",
    )(pos, flat_ids, *arrived)


def label_kernel(*refs):
    sum_refs, (cent_ref, embed_ref, member_ref, mixed_ref) = refs[:-4], refs[-4:]
    sums = []
    for at in range(0, len(sum_refs), SIDE):
        sums.append(sum_refs[at][...] + sum_refs[at + 1][...] + sum_refs[at + 2][...] + sum_refs[at + 3][...])
    sums = jnp.concatenate(sums, axis=1)
    embed = (sums * lax.rsqrt(jnp.mean(sums * sums, axis=1, keepdims=True) + EPSILON)).astype(jnp.bfloat16)
    embed_ref[...] = embed
    scores = lax.dot_general(embed, cent_ref[...], (((1,), (1,)), ((), ())), preferred_element_type=jnp.float32)
    lifted = jnp.exp(scores - jnp.max(scores, axis=1, keepdims=True))
    member = (lifted / jnp.sum(lifted, axis=1, keepdims=True)).astype(jnp.bfloat16)
    member_ref[...] = member
    mixed_ref[...] = jnp.dot(member, cent_ref[...], preferred_element_type=jnp.float32).astype(jnp.bfloat16)


def label_side(sums, centroids):
    rows = sums[0].shape[0]
    clusters, feat = centroids.shape
    tile = LABEL_TILE
    by_row = lambda i: (i, 0)
    return pl.pallas_call(
        label_kernel,
        out_shape=(
            jax.ShapeDtypeStruct((rows, feat), jnp.bfloat16),
            jax.ShapeDtypeStruct((rows, clusters), jnp.bfloat16),
            jax.ShapeDtypeStruct((rows, feat), jnp.bfloat16),
        ),
        grid=(rows // tile,),
        in_specs=[pl.BlockSpec((tile, s.shape[1]), by_row) for s in sums]
        + [pl.BlockSpec((clusters, feat), lambda i: (0, 0))],
        out_specs=(
            pl.BlockSpec((tile, feat), by_row),
            pl.BlockSpec((tile, clusters), by_row),
            pl.BlockSpec((tile, feat), by_row),
        ),
        name="label_side",
    )(*sums, centroids)


def target_kernel(group, count_ref, slot_ref, inst_ref, lab_ref, *refs):
    bits_refs, mixed_refs, (out_ref, total) = refs[:group], refs[group : 2 * group], refs[2 * group :]
    at = pl.program_id(0) * group

    @pl.when(at == 0)
    def _():
        total[...] = jnp.zeros_like(total)

    @pl.when(at < count_ref[0])
    def _():
        for k in range(group):
            used = (at + k < count_ref[0]).astype(jnp.int32)
            incidence = (bits_refs[k][0] * used).astype(jnp.float32).astype(jnp.bfloat16)
            part = jnp.dot(incidence, mixed_refs[k][0], preferred_element_type=jnp.float32)
            total[inst_ref[at + k]] += part

    @pl.when(at + group == group * pl.num_programs(0))
    def _():
        for g in range(total.shape[0]):
            raw = total[g]
            scale = lax.rsqrt(jnp.mean(raw * raw, axis=1, keepdims=True) + EPSILON)
            out_ref[g] = (raw * scale).astype(jnp.bfloat16)


def target_blocks(slots, insts, labs, n_used, block_bits, mixed_blocks, n_inst):
    n_slots, block, _ = block_bits.shape
    feat = mixed_blocks.shape[-1]
    group = TARGET_GROUP

    def pick(table, k):
        def index(g, n, *tables):
            return (tables[table][jnp.minimum(g, (jnp.maximum(n[0], 1) - 1) // group) * group + k], 0, 0)

        return index

    return pl.pallas_call(
        functools.partial(target_kernel, group),
        out_shape=jax.ShapeDtypeStruct((n_inst, block, feat), jnp.bfloat16),
        grid_spec=pltpu.PrefetchScalarGridSpec(
            num_scalar_prefetch=4,
            grid=(n_slots // group,),
            in_specs=[pl.BlockSpec((1, block, block), pick(0, k)) for k in range(group)]
            + [pl.BlockSpec((1, block, feat), pick(2, k)) for k in range(group)],
            out_specs=pl.BlockSpec((n_inst, block, feat), lambda g, *tables: (0, 0, 0)),
            scratch_shapes=[pltpu.VMEM((n_inst, block, feat), jnp.float32)],
        ),
        name="target_blocks",
    )(n_used, slots, insts, labs, *([block_bits] * group), *([mixed_blocks] * group))


def body(features, inst_ids, lab_ids, counts, block_bits, centroids):
    columns, cap = inst_ids.shape
    block = block_bits.shape[-1]
    feat = features.shape[1]
    planes = lax.axis_size("dp")
    inst_blocks = features.reshape(-1, block, feat)
    inst_flat = inst_ids.reshape(-1)
    d = lax.axis_index("dp")
    e = lax.axis_index("label")
    pos = jnp.stack([e // SIDE, e % SIDE, d // 2, d % 2]).astype(jnp.int32)

    filled = jnp.arange(cap)[None, :] < counts[:, None]
    tagged_ids = jnp.where(filled, lab_ids, -1).reshape(SIDE, SIDE, cap)
    tagged_ids = jnp.roll(tagged_ids, (-(e // SIDE), -(e % SIDE)), (0, 1))
    near = [shift_first(tagged_ids[step], step) if step else tagged_ids[0] for step in range(SIDE)]
    near = jnp.stack(near, axis=1)
    near = [shift_second(near[step], step) if step else near[0] for step in range(SIDE)]

    share = centroids.shape[0] // planes
    own_rows = lax.dynamic_slice_in_dim(centroids, d * share, share, 0)
    all_rows = lax.all_gather(own_rows, ("label", "dp"), axis=0, tiled=True)

    shifts = (shift_first, shift_second)
    sums = []
    stage = {}
    for part, groups in MAKE:
        made = partial_blocks(pos, inst_flat, block_bits, inst_blocks, groups, part)
        for (first_axis, outer), blocks in zip(groups, made):
            stage[part, first_axis, outer] = shifts[first_axis](blocks, outer) if outer else blocks
    for part in range(len(SPLITS)):
        arrived = []
        for first_axis in range(2):
            received = [stage[part, first_axis, step] for step in range(SIDE)]
            arrived += received
            packed = pack_groups(received)
            for outer, group in enumerate(packed, start=1):
                arrived.append(shifts[1 - first_axis](group, outer))
        if part == 0:
            near, arrived = lax.optimization_barrier((near, arrived))
            flat_ids = jnp.stack(near, axis=1).reshape(-1)
        keep, send = sum_blocks(pos, flat_ids, arrived, planes * LB_DEV)
        other = swap_core(send)
        for step in range(SIDE):
            rows = slice(step * LB_DEV, (step + 1) * LB_DEV)
            piece = (keep[rows] + other[rows]).reshape(LB_DEV * block, -1)
            sums.append(shift_plane(piece, step) if step else piece)
    label_embed, membership, mixed = label_side(sums, all_rows)
    mixed_all = lax.all_gather(mixed, ("dp", "label"), axis=0, tiled=True)

    column = jnp.arange(columns, dtype=jnp.int32)[:, None]
    global_ids = ((lab_ids // LB_DEV * columns + column) * LB_DEV + lab_ids % LB_DEV).reshape(-1)
    used = filled.reshape(-1)
    place = jnp.where(used, jnp.cumsum(used) - 1, used.size)
    slots = jnp.arange(used.size, dtype=jnp.int32)
    chosen = (place[None, :] == slots[:, None]).astype(jnp.int32)
    tables = [jnp.sum(chosen * table[None, :], axis=1) for table in (slots, inst_flat, global_ids)]
    n_used = jnp.sum(used, dtype=jnp.int32).reshape(1)
    targets = target_blocks(
        *tables, n_used, block_bits.reshape(-1, block, block), mixed_all.reshape(-1, block, feat), inst_blocks.shape[0]
    )
    return (label_embed, membership, targets.reshape(features.shape))


def solution(mesh):
    in_specs = (
        P(("dp", "label"), None),
        P(("dp", "label"), None),
        P(("dp", "label"), None),
        P(("dp", "label")),
        P(("dp", "label"), None, None, None),
        P("label", None),
    )
    out_specs = (P(("dp", "label"), None), P(("dp", "label"), None), P(("dp", "label"), None))
    return jax.shard_map(body, mesh=mesh, in_specs=in_specs, out_specs=out_specs, check_vma=False)
```

```python
import functools

import jax
import jax.numpy as jnp
from jax import lax
from jax.experimental import pallas as pl
from jax.experimental.pallas import tpu as pltpu
from jax.sharding import PartitionSpec as P


LB_DEV = 2
EPSILON = 1e-05
SUM_STEPS = 2
LABEL_TILE = 256
TARGET_GROUP = 8
SIDE = 4
SPLITS = ((256, 0), (128, 4))


MAKE = (
    (0, ((0, 2), (1, 2))),
    (0, ((0, 1), (0, 3))),
    (0, ((1, 1), (1, 3))),
    (1, ((0, 2), (0, 1), (0, 3))),
    (1, ((1, 2), (1, 1), (1, 3))),
    (0, ((0, 0), (1, 0))),
    (1, ((0, 0), (1, 0))),
)


def mod4(value):
    return jnp.bitwise_and(value, SIDE - 1)


def shift_first(array, step):
    pairs = [(a * SIDE + b, (a + step) % SIDE * SIDE + b) for a in range(SIDE) for b in range(SIDE)]
    return lax.ppermute(array, "label", pairs)


def shift_second(array, step):
    pairs = [(a * SIDE + b, a * SIDE + (b + step) % SIDE) for a in range(SIDE) for b in range(SIDE)]
    return lax.ppermute(array, "label", pairs)


def shift_plane(array, step):
    pairs = [(a * 2 + b, (a + step) % SIDE * 2 + b) for a in range(SIDE) for b in range(2)]
    return lax.ppermute(array, "dp", pairs)


def swap_core(array):
    return lax.ppermute(array, "dp", [(a * 2 + b, a * 2 + 1 - b) for a in range(SIDE) for b in range(2)])


def partial_kernel(cap, groups, axes, pos_ref, inst_ref, *refs):
    bits_refs, refs = refs[: len(groups)], refs[len(groups) :]
    feat_refs, out_refs = dict(zip(axes, refs)), refs[len(axes) :]
    for (first_axis, outer), bits_ref, out_ref in zip(groups, bits_refs, out_refs):
        fixed = mod4(pos_ref[first_axis] + outer)
        for inner in range(SIDE):
            other = mod4(pos_ref[1 - first_axis] + inner)
            column = fixed * SIDE + other if first_axis == 0 else other * SIDE + fixed
            for k in range(cap):
                incidence = bits_ref[0, other, k] if first_axis == 0 else bits_ref[other, 0, k]
                part = lax.dot_general(
                    incidence.astype(jnp.float32).astype(jnp.bfloat16),
                    feat_refs[first_axis][inst_ref[column * cap + k]],
                    (((0,), (0,)), ((), ())),
                    preferred_element_type=jnp.float32,
                )
                out_ref[inner, k] = part.astype(jnp.bfloat16)


def partial_blocks(pos, inst_flat, block_bits, inst_blocks, groups, part):
    _, cap, block, _ = block_bits.shape
    n_inst = inst_blocks.shape[0]
    width, start = SPLITS[part]
    grid_bits = block_bits.reshape(SIDE, SIDE, cap, block, block)
    axes = tuple(sorted({first_axis for first_axis, _ in groups}))
    bits_specs = []
    for first_axis, outer in groups:
        if first_axis == 0:
            shape, index = (1, SIDE), lambda g, p, i, outer=outer: (mod4(p[0] + outer), 0, 0, 0, 0)
        else:
            shape, index = (SIDE, 1), lambda g, p, i, outer=outer: (0, mod4(p[1] + outer), 0, 0, 0)
        bits_specs.append(pl.BlockSpec(shape + (cap, block, block), index))
    feat_specs = [
        pl.BlockSpec((n_inst, block, width), lambda g, p, i, at=start + axis: (0, 0, at)) for axis in axes
    ]
    out = jax.ShapeDtypeStruct((SIDE, cap, block, width), jnp.bfloat16)
    return pl.pallas_call(
        functools.partial(partial_kernel, cap, groups, axes),
        out_shape=(out,) * len(groups),
        grid_spec=pltpu.PrefetchScalarGridSpec(
            num_scalar_prefetch=2,
            grid=(1,),
            in_specs=bits_specs + feat_specs,
            out_specs=(pl.BlockSpec(out.shape, lambda g, p, i: (0, 0, 0, 0)),) * len(groups),
        ),
        cost_estimate=pl.CostEstimate(
            flops=2 * len(groups) * SIDE * cap * block * block * width,
            bytes_accessed=len(groups) * (4 << 20),
            transcendentals=0,
        ),
        name="partial_blocks",
    )(pos, inst_flat, *([grid_bits] * len(groups)), *([inst_blocks] * len(axes)))


def pack_kernel(*refs):
    ins, outs = refs[:SIDE], refs[SIDE:]
    for outer, out_ref in enumerate(outs, start=1):
        for step, ref in enumerate(ins):
            out_ref[step] = ref[outer]


def pack_groups(received):
    shape = received[0].shape
    whole = pl.BlockSpec(shape, lambda i: (0, 0, 0, 0))
    return pl.pallas_call(
        pack_kernel,
        out_shape=(jax.ShapeDtypeStruct(shape, received[0].dtype),) * (SIDE - 1),
        grid=(1,),
        in_specs=[whole] * len(received),
        out_specs=(whole,) * (SIDE - 1),
        cost_estimate=pl.CostEstimate(flops=0, bytes_accessed=8 << 20, transcendentals=0),
        compiler_params=pltpu.CompilerParams(vmem_limit_bytes=20 << 20),
        name="pack_groups",
    )(*received)


def sum_kernel(cap, width, pos_ref, ids_ref, *refs):
    arrived, (keep_ref, send_ref, total) = refs[: 4 * SIDE - 2], refs[4 * SIDE - 2 :]
    half = keep_ref.shape[0]
    per_step = SIDE // SUM_STEPS
    at = pl.program_id(0) * per_step

    @pl.when(at == 0)
    def _():
        total[...] = jnp.zeros_like(total)

    def add(first_axis, outer, inner, ref, row_at):
        step = (inner, outer) if first_axis == 0 else (outer, inner)
        sender = step[0] * SIDE + step[1]
        for k in range(cap):
            target = ids_ref[sender * cap + k]
            away = jnp.bitwise_xor(jnp.bitwise_and(target >> 1, 1), pos_ref[3])
            row = away * half + mod4((target >> 2) - pos_ref[2]) * LB_DEV + jnp.bitwise_and(target, 1)
            row = jnp.where(target >= 0, row, 2 * half)
            columns = pl.ds(first_axis * width, width)
            total[row, :, columns] += ref[row_at, k].astype(jnp.float32)

    for first_axis in range(2):
        refs_here = arrived[first_axis * (2 * SIDE - 1) : (first_axis + 1) * (2 * SIDE - 1)]
        for step in range(SIDE):

            @pl.when(at == step // per_step * per_step)
            def _():
                add(first_axis, 0, step, refs_here[step], 0)

        for outer in range(1, SIDE):
            for step in range(per_step):
                add(first_axis, outer, at + step, refs_here[SIDE - 1 + outer], step)

    @pl.when(at == SIDE - per_step)
    def _():
        keep_ref[...] = total[:half]
        send_ref[...] = total[half : 2 * half]


def sum_blocks(pos, flat_ids, arrived, col_blocks):
    _, cap, block, width = arrived[0].shape
    half = jax.ShapeDtypeStruct((col_blocks // 2, block, 2 * width), jnp.float32)
    whole = pl.BlockSpec(half.shape, lambda j, p, i: (0, 0, 0))
    own = pl.BlockSpec((1, cap, block, width), lambda j, p, i: (0, 0, 0, 0))
    far = pl.BlockSpec((SIDE // SUM_STEPS, cap, block, width), lambda j, p, i: (j, 0, 0, 0))
    return pl.pallas_call(
        functools.partial(sum_kernel, cap, width),
        out_shape=(half, half),
        grid_spec=pltpu.PrefetchScalarGridSpec(
            num_scalar_prefetch=2,
            grid=(SUM_STEPS,),
            in_specs=([own] * SIDE + [far] * (SIDE - 1)) * 2,
            out_specs=(whole, whole),
            scratch_shapes=[pltpu.VMEM((col_blocks + 1, block, 2 * width), jnp.float32)],
        ),
        cost_estimate=pl.CostEstimate(
            flops=SIDE * SIDE * cap * block * 2 * width, bytes_accessed=12 << 20, transcendentals=0
        ),
        compiler_params=pltpu.CompilerParams(vmem_limit_bytes=26 << 20),
        name="sum_blocks",
    )(pos, flat_ids, *arrived)


def label_kernel(*refs):
    sum_refs, (cent_ref, embed_ref, member_ref, mixed_ref) = refs[:-4], refs[-4:]
    sums = []
    for at in range(0, len(sum_refs), SIDE):
        sums.append(sum_refs[at][...] + sum_refs[at + 1][...] + sum_refs[at + 2][...] + sum_refs[at + 3][...])
    sums = jnp.concatenate(sums, axis=1)
    embed = (sums * lax.rsqrt(jnp.mean(sums * sums, axis=1, keepdims=True) + EPSILON)).astype(jnp.bfloat16)
    embed_ref[...] = embed
    scores = lax.dot_general(embed, cent_ref[...], (((1,), (1,)), ((), ())), preferred_element_type=jnp.float32)
    lifted = jnp.exp(scores - jnp.max(scores, axis=1, keepdims=True))
    member = (lifted / jnp.sum(lifted, axis=1, keepdims=True)).astype(jnp.bfloat16)
    member_ref[...] = member
    mixed_ref[...] = jnp.dot(member, cent_ref[...], preferred_element_type=jnp.float32).astype(jnp.bfloat16)


def label_side(sums, centroids):
    rows = sums[0].shape[0]
    clusters, feat = centroids.shape
    tile = LABEL_TILE
    by_row = lambda i: (i, 0)
    return pl.pallas_call(
        label_kernel,
        out_shape=(
            jax.ShapeDtypeStruct((rows, feat), jnp.bfloat16),
            jax.ShapeDtypeStruct((rows, clusters), jnp.bfloat16),
            jax.ShapeDtypeStruct((rows, feat), jnp.bfloat16),
        ),
        grid=(rows // tile,),
        in_specs=[pl.BlockSpec((tile, s.shape[1]), by_row) for s in sums]
        + [pl.BlockSpec((clusters, feat), lambda i: (0, 0))],
        out_specs=(
            pl.BlockSpec((tile, feat), by_row),
            pl.BlockSpec((tile, clusters), by_row),
            pl.BlockSpec((tile, feat), by_row),
        ),
        compiler_params=pltpu.CompilerParams(vmem_limit_bytes=32 << 20),
        name="label_side",
    )(*sums, centroids)


def target_kernel(group, count_ref, slot_ref, inst_ref, lab_ref, *refs):
    bits_refs, mixed_refs = refs[:group], refs[group : 2 * group]
    out_ref, total, rows, sems = refs[2 * group :]
    at = pl.program_id(0) * group

    @pl.when(at == 0)
    def _():
        total[...] = jnp.zeros_like(total)

    @pl.when(at < count_ref[0])
    def _():
        for k in range(group):
            used = (at + k < count_ref[0]).astype(jnp.int32)
            incidence = (bits_refs[k][0] * used).astype(jnp.float32).astype(jnp.bfloat16)
            part = jnp.dot(incidence, mixed_refs[k][0], preferred_element_type=jnp.float32)
            total[inst_ref[at + k]] += part

    @pl.when(at + group == group * pl.num_programs(0))
    def _():
        for g in range(total.shape[0]):
            raw = total[g]
            scale = lax.rsqrt(jnp.mean(raw * raw, axis=1, keepdims=True) + EPSILON)
            rows[g] = (raw * scale).astype(jnp.bfloat16)
            pltpu.make_async_copy(rows.at[g], out_ref.at[g], sems.at[g]).start()
        for g in range(total.shape[0]):
            pltpu.make_async_copy(rows.at[g], out_ref.at[g], sems.at[g]).wait()


def target_blocks(slots, insts, labs, n_used, block_bits, mixed_blocks, n_inst):
    n_slots, block, _ = block_bits.shape
    feat = mixed_blocks.shape[-1]
    group = TARGET_GROUP

    def pick(table, k):
        def index(g, n, *tables):
            return (tables[table][jnp.minimum(g, (jnp.maximum(n[0], 1) - 1) // group) * group + k], 0, 0)

        return index

    return pl.pallas_call(
        functools.partial(target_kernel, group),
        out_shape=jax.ShapeDtypeStruct((n_inst, block, feat), jnp.bfloat16),
        grid_spec=pltpu.PrefetchScalarGridSpec(
            num_scalar_prefetch=4,
            grid=(n_slots // group,),
            in_specs=[pl.BlockSpec((1, block, block), pick(0, k)) for k in range(group)]
            + [pl.BlockSpec((1, block, feat), pick(2, k)) for k in range(group)],
            out_specs=pl.BlockSpec(memory_space=pl.ANY),
            scratch_shapes=[
                pltpu.VMEM((n_inst, block, feat), jnp.float32),
                pltpu.VMEM((n_inst, block, feat), jnp.bfloat16),
                pltpu.SemaphoreType.DMA((n_inst,)),
            ],
        ),
        name="target_blocks",
    )(n_used, slots, insts, labs, *([block_bits] * group), *([mixed_blocks] * group))


def body(features, inst_ids, lab_ids, counts, block_bits, centroids):
    columns, cap = inst_ids.shape
    block = block_bits.shape[-1]
    feat = features.shape[1]
    planes = lax.axis_size("dp")
    inst_blocks = features.reshape(-1, block, feat)
    inst_flat = inst_ids.reshape(-1)
    d = lax.axis_index("dp")
    e = lax.axis_index("label")
    pos = jnp.stack([e // SIDE, e % SIDE, d // 2, d % 2]).astype(jnp.int32)

    filled = jnp.arange(cap)[None, :] < counts[:, None]
    tagged_ids = jnp.where(filled, lab_ids, -1).reshape(SIDE, SIDE, cap)
    tagged_ids = jnp.roll(tagged_ids, (-(e // SIDE), -(e % SIDE)), (0, 1))
    near = [shift_first(tagged_ids[step], step) if step else tagged_ids[0] for step in range(SIDE)]
    near = jnp.stack(near, axis=1)
    near = [shift_second(near[step], step) if step else near[0] for step in range(SIDE)]

    shifts = (shift_first, shift_second)
    sums = []
    stage = {}
    for at, (part, groups) in enumerate(MAKE):
        made = partial_blocks(pos, inst_flat, block_bits, inst_blocks, groups, part)
        if at == 2:
            made, centroids = lax.optimization_barrier((made, centroids))
        for (first_axis, outer), blocks in zip(groups, made):
            stage[part, first_axis, outer] = shifts[first_axis](blocks, outer) if outer else blocks
    share = centroids.shape[0] // planes
    own_rows = lax.dynamic_slice_in_dim(centroids, d * share, share, 0)
    all_rows = lax.all_gather(own_rows, ("label", "dp"), axis=0, tiled=True)

    for part in range(len(SPLITS)):
        arrived = []
        for first_axis in range(2):
            received = [stage[part, first_axis, step] for step in range(SIDE)]
            arrived += received
            packed = pack_groups(received)
            for outer, group in enumerate(packed, start=1):
                arrived.append(shifts[1 - first_axis](group, outer))
        if part == 0:
            near, arrived = lax.optimization_barrier((near, arrived))
            flat_ids = jnp.stack(near, axis=1).reshape(-1)
        keep, send = sum_blocks(pos, flat_ids, arrived, planes * LB_DEV)
        other = swap_core(send)
        if part == len(SPLITS) - 1:
            other, all_rows = lax.optimization_barrier((other, all_rows))
        for step in range(SIDE):
            rows = slice(step * LB_DEV, (step + 1) * LB_DEV)
            piece = (keep[rows] + other[rows]).reshape(LB_DEV * block, -1)
            sums.append(shift_plane(piece, step) if step else piece)
    label_embed, membership, mixed = label_side(sums, all_rows)
    mixed_all = lax.all_gather(mixed, ("dp", "label"), axis=0, tiled=True)

    column = jnp.arange(columns, dtype=jnp.int32)[:, None]
    global_ids = ((lab_ids // LB_DEV * columns + column) * LB_DEV + lab_ids % LB_DEV).reshape(-1)
    used = filled.reshape(-1)
    place = jnp.where(used, jnp.cumsum(used) - 1, used.size)
    slots = jnp.arange(used.size, dtype=jnp.int32)
    chosen = (place[None, :] == slots[:, None]).astype(jnp.int32)
    tables = [jnp.sum(chosen * table[None, :], axis=1) for table in (slots, inst_flat, global_ids)]
    n_used = jnp.sum(used, dtype=jnp.int32).reshape(1)
    targets = target_blocks(
        *tables, n_used, block_bits.reshape(-1, block, block), mixed_all.reshape(-1, block, feat), inst_blocks.shape[0]
    )
    return (label_embed, membership, targets.reshape(features.shape))


def solution(mesh):
    in_specs = (
        P(("dp", "label"), None),
        P(("dp", "label"), None),
        P(("dp", "label"), None),
        P(("dp", "label")),
        P(("dp", "label"), None, None, None),
        P("label", None),
    )
    out_specs = (P(("dp", "label"), None), P(("dp", "label"), None), P(("dp", "label"), None))
    return jax.shard_map(body, mesh=mesh, in_specs=in_specs, out_specs=out_specs, check_vma=False)
```
